32 devices in a mesh: tm: 2 (over y), space: 16 (over z, x, core).
Axes of the slice: x: 2, y: 2, z: 4, core: 2. Of those that a mesh axis runs over, the one named last changes fastest.
Arguments:
- control: float32 [32, 51200], P(('tm', 'space')), may hold values from -4 to 4
- spectrum: float32 [51200], replicated, may hold values from 0.2 to 2
- perturb: bfloat16 [4, 32, 4, 51200], P('tm', None, None, 'space'), may hold values from -1 to 1
- obs_index: int32 [4, 32768], P('tm', 'space'), may hold values from 0 to 12799
- innovation: float32 [4, 32768], P('tm', 'space'), may hold values from -10 to 10
- obs_sigma: float32 [4, 32768], P('tm', 'space'), may hold values from 0.5 to 2
- qc_class: int32 [4, 32768], P('tm', 'space'), may hold values from 0 to 2
Outputs:
- control_out: float32 [32, 51200], P(('tm', 'space'))
- cost_list: float32 [1], replicated
The draws below stay inside these ranges and needn't reach their ends.
Inputs may be any that keep to these rules, and one draw needn't show every extreme that they name: `obs_index`: observation o of block o // 2048 observes the cell level * 3200 + point, the point counted within the block's piece of the grid; repeats may occur.
All inputs are finite; a program needn't handle non-finite values.
Results may differ from the reference program's by a relative error of at most 0.0034.
Values may be sent and summed in bfloat16 or wider, within the bound.
A program may use at most 128 MiB of HBM per device.

```python
import math
import jax
import jax.numpy as jnp
from jax import lax

GX = 320
GY = 160
LEV = 4
ITERS = 1
OBS_DEV = 2048
TIMES = 4
MEMBERS = 32
NOBS = 32768
N_SPACE = 16


def set_ends(entries, stream_key, smallest, top_value):
    longest = entries.shape.index(max(entries.shape))
    spots = []
    for shift in (0, 1):
        where = [jax.random.randint(jax.random.fold_in(stream_key, axis), (), 0, length) for axis, length in enumerate(entries.shape)]
        where[longest] = (where[longest] + shift) % entries.shape[longest]
        spots.append(tuple(where))
    return entries.at[spots[0]].set(smallest).at[spots[1]].set(top_value)


def shard_levels(own_key, dims, shards, low, high):
    def one(position, shards_of):
        draws = jax.random.uniform(jax.random.fold_in(jax.random.fold_in(own_key, 6), position), (shards_of,), jnp.float32, low / len(shards), high / len(shards))
        return jnp.repeat(jnp.exp(draws), dims[position] // shards_of).reshape((-1,) + (1,) * (len(dims) - position - 1))

    factor_of = one(*shards[0])
    for cut in shards[1:]:
        factor_of = factor_of * one(*cut)
    return factor_of


def noise(key, shape, spread, most, shards=(), held_as=jnp.bfloat16):
    drawn = spread * jax.random.normal(key, shape, jnp.float32)
    if shards:
        drawn = drawn * shard_levels(key, shape, shards, -0.22, 0.18)
    return jnp.clip(drawn, -most, most).astype(held_as)


def setup_inputs(seed: int = 0) -> dict:
    key_list = jax.random.split(jax.random.key(seed), 8)
    return {
        "control": noise(key_list[0], (MEMBERS, GX * GY), 0.5, 4.0, ((0, 32),), jnp.float32),
        "spectrum": jnp.clip(jnp.exp(jax.random.uniform(key_list[1], (GX * GY,), jnp.float32, math.log(0.2), math.log(2.0))), 0.2, 2.0),
        "perturb": noise(key_list[2], (TIMES, MEMBERS, LEV, GX * GY), MEMBERS ** -0.5, 1.0, ((0, 2), (3, 16))),
        "obs_index": set_ends(jax.random.randint(key_list[3], (TIMES, NOBS), 0, LEV * (GX * GY // N_SPACE)), jax.random.fold_in(key_list[3], 1), 0, (LEV * (GX * GY // N_SPACE)) - 1).astype(jnp.int32),
        "innovation": noise(key_list[4], (TIMES, NOBS), 2.0, 10.0, ((0, 2), (1, 16)), jnp.float32),
        "obs_sigma": jnp.clip(jnp.exp(math.log(2.0) - 1.3862944 * jax.random.uniform(key_list[5], (TIMES, NOBS), jnp.float32) ** shard_levels(key_list[5], (TIMES, NOBS), ((0, 2), (1, 16)), -0.2, 0.2)), 0.5, 2.0),
        "qc_class": set_ends(jax.random.randint(key_list[6], (TIMES, NOBS), 0, 3), jax.random.fold_in(key_list[6], 1), 0, 2).astype(jnp.int32),
    }


def lookup_tables(segment_length):
    wave_num = jnp.arange(segment_length, dtype=jnp.float32)[:, None]
    grid_positions = jnp.arange(segment_length, dtype=jnp.float32)[None, :]
    basis = jnp.cos(jnp.pi * (grid_positions + 0.5) * wave_num / segment_length) * jnp.sqrt(2.0 / segment_length)
    return jnp.where(wave_num == 0, basis * jnp.sqrt(0.5), basis)

def synthesize(control, spectrum, basis_x, basis_y):
    coeffs = (control * spectrum[None, :]).reshape(control.shape[0], GX, GY)
    middle = jnp.einsum('kn,mkl->mnl', basis_x, coeffs, precision=lax.Precision.HIGHEST)
    result = jnp.einsum('mnl,lp->mnp', middle, basis_y, precision=lax.Precision.HIGHEST)
    return result.reshape(control.shape[0], GX * GY)

def analyze(adjoint, spectrum, basis_x, basis_y):
    state_fields = adjoint.reshape(adjoint.shape[0], GX, GY)
    middle = jnp.einsum('kn,mnp->mkp', basis_x, state_fields, precision=lax.Precision.HIGHEST)
    result = jnp.einsum('mkp,lp->mkl', middle, basis_y, precision=lax.Precision.HIGHEST)
    return result.reshape(adjoint.shape[0], GX * GY) * spectrum[None, :]

def reference(control, spectrum, perturb, obs_index, innovation, obs_sigma, qc_class):
    basis_x = lookup_tables(GX)
    basis_y = lookup_tables(GY)
    grid_total = GX * GY
    piece_len = grid_total // N_SPACE
    block_ids = (jnp.arange(innovation.shape[1], dtype=jnp.int32) // OBS_DEV).astype(jnp.int32)
    cell_index = obs_index // piece_len * grid_total + block_ids[None, :] * piece_len + obs_index % piece_len
    cell_index = cell_index.astype(jnp.int32)
    radius = jnp.where(qc_class == 0, 4.0, jnp.where(qc_class == 1, 2.0, 1.0)).astype(jnp.float32)
    cost_list = []

    def scatter_cells(indices, values):
        return jnp.zeros((LEV * grid_total,), jnp.float32).at[indices].add(values)
    for iteration in range(ITERS):
        member_field = synthesize(control, spectrum, basis_x, basis_y).astype(jnp.bfloat16)
        field_wide = member_field.astype(jnp.float32)

        def forward(slot_data):
            return jnp.einsum('mlg,mg->lg', slot_data.astype(jnp.float32), field_wide).reshape(-1)
        increment = lax.map(forward, perturb)
        modelled = jnp.take_along_axis(increment, cell_index, axis=1)
        scaled = (modelled - innovation) / obs_sigma
        scaled_sq = scaled * scaled / (radius * radius)
        obs_cost = jnp.sum(0.5 * radius * radius * jnp.log1p(scaled_sq))
        back_cost = 0.5 * jnp.sum(control * control)
        obs_grad = scaled / ((1.0 + scaled_sq) * obs_sigma)
        control_update = jax.vmap(scatter_cells)(cell_index, obs_grad).astype(jnp.bfloat16)

        def backward(running, pair):
            slot_data, slot_update = pair
            term = jnp.einsum('mlg,lg->mg', slot_data.astype(jnp.float32), slot_update.reshape(LEV, grid_total).astype(jnp.float32))
            return (running + term, None)
        adjoint, unused = lax.scan(backward, jnp.zeros(control.shape, jnp.float32), (perturb, control_update))
        gradient = control + analyze(adjoint, spectrum, basis_x, basis_y)
        grad_sq = jnp.sum(gradient * gradient)
        total_cost = back_cost + obs_cost
        step_size = 0.5 * total_cost / (grad_sq + 1e-06)
        control = control - step_size * gradient
        cost_list.append(total_cost)
    return (control, jnp.stack(cost_list))
```

```python
import functools

import jax
import jax.numpy as jnp
import ml_dtypes
import numpy as np
from jax import lax
from jax.experimental import pallas as pl
from jax.experimental.pallas import tpu as pltpu
from jax.sharding import PartitionSpec as P

GX = 320
GY = 160


def lookup_tables(segment_length):
    wave_num = jnp.arange(segment_length, dtype=jnp.float32)[:, None]
    grid_positions = jnp.arange(segment_length, dtype=jnp.float32)[None, :]
    basis = jnp.cos(jnp.pi * (grid_positions + 0.5) * wave_num / segment_length) * jnp.sqrt(
        2.0 / segment_length
    )
    return jnp.where(wave_num == 0, basis * jnp.sqrt(0.5), basis)


def synthesize(control, spectrum, basis_x, basis_y):
    coeffs = (control * spectrum[None, :]).reshape(control.shape[0], GX, GY)
    middle = jnp.einsum("kn,mkl->mnl", basis_x, coeffs, precision=lax.Precision.HIGHEST)
    result = jnp.einsum("mnl,lp->mnp", middle, basis_y, precision=lax.Precision.HIGHEST)
    return result.reshape(control.shape[0], GX * GY)


def analyze(adjoint, spectrum, basis_x, basis_y):
    state_fields = adjoint.reshape(adjoint.shape[0], GX, GY)
    middle = jnp.einsum("kn,mnp->mkp", basis_x, state_fields, precision=lax.Precision.HIGHEST)
    result = jnp.einsum("mkp,lp->mkl", middle, basis_y, precision=lax.Precision.HIGHEST)
    return result.reshape(adjoint.shape[0], GX * GY) * spectrum[None, :]


def per_device(control, spectrum, perturb, obs_index, innovation, obs_sigma, qc_class):
    basis_x = lookup_tables(GX)
    basis_y = lookup_tables(GY)
    slot_count = perturb.shape[0]
    levels = perturb.shape[2]
    piece_len = perturb.shape[3]
    radius = jnp.where(qc_class == 0, 4.0, jnp.where(qc_class == 1, 2.0, 1.0)).astype(jnp.float32)

    def scatter_cells(indices, values):
        return jnp.zeros((levels * piece_len,), jnp.float32).at[indices].add(values)

    member_field = synthesize(control, spectrum, basis_x, basis_y).astype(jnp.bfloat16)
    pieces = lax.all_to_all(member_field, "space", split_axis=1, concat_axis=0, tiled=True)
    selected_entries = perturb
    increment = jnp.einsum(
        "dzab,zb->dab",
        selected_entries,
        lax.all_gather(pieces, "tm", axis=0, tiled=True),
        preferred_element_type=jnp.float32,
    )
    cells_flat = increment.reshape(slot_count, levels * piece_len)
    modelled = jnp.take_along_axis(cells_flat, obs_index, axis=1)
    scaled = (modelled - innovation) / obs_sigma
    scaled_sq = scaled * scaled / (radius * radius)
    obs_part = jnp.sum(0.5 * radius * radius * jnp.log1p(scaled_sq))
    back_part = 0.5 * jnp.sum(control * control)
    obs_grad = scaled / ((1.0 + scaled_sq) * obs_sigma)
    control_update = jax.vmap(scatter_cells)(obs_index, obs_grad).astype(jnp.bfloat16)
    control_update = control_update.reshape(slot_count, levels, piece_len)
    selected_entries = perturb
    summed_rows = lax.psum_scatter(
        jnp.einsum(
            "qiyr,qyr->ir", selected_entries, control_update, preferred_element_type=jnp.float32
        ).astype(jnp.bfloat16),
        "tm",
        scatter_dimension=0,
        tiled=True,
    ).astype(jnp.float32)
    adjoint = lax.all_to_all(
        summed_rows.astype(jnp.bfloat16), "space", split_axis=0, concat_axis=1, tiled=True
    ).astype(summed_rows.dtype)
    gradient = control + analyze(adjoint, spectrum, basis_x, basis_y)
    grad_part = jnp.sum(gradient * gradient)
    obs_cost, back_cost = lax.psum((obs_part, back_part), ("tm", "space"))
    grad_sq = lax.psum(grad_part, ("tm", "space"))
    total_cost = back_cost + obs_cost
    step_size = 0.5 * total_cost / (grad_sq + 1e-06)
    control = control - step_size * gradient
    cost_list = [total_cost]
    return (control, jnp.stack(cost_list))


LANES = 128
FOLD = 4
MESH_ID = pl.DeviceIdType.MESH
F32 = jnp.float32
BF16 = jnp.bfloat16


def basis64(n):
    k = np.arange(n, dtype=np.float64)[:, None]
    x = np.arange(n, dtype=np.float64)[None, :]
    c = np.sqrt(2.0 / n) * np.cos(np.pi * (x + 0.5) * k / n)
    c[0] *= np.sqrt(0.5)
    return c.astype(np.float32)


def two_parts(c):
    hi = c.astype(ml_dtypes.bfloat16)
    lo = (c - hi.astype(np.float32)).astype(ml_dtypes.bfloat16)
    return np.stack([hi, lo])


def folded_bases():
    cx, cy = basis64(GX), basis64(GY)
    order = np.arange(GX).reshape(GX // FOLD, FOLD).T.reshape(-1)
    cxp = cx[order][:, order]
    return [two_parts(np.ascontiguousarray(a)) for a in (cxp, cxp.T, cy, cy.T)]


def split2(x):
    hi = x.astype(BF16)
    return hi, (x - hi.astype(F32)).astype(BF16)


def split3(x):
    a = x.astype(BF16).astype(F32)
    b = (x - a).astype(BF16).astype(F32)
    return a, b, x - a - b


def mm(a, b):
    return jnp.dot(a, b, preferred_element_type=F32)


def dot_right(x, c_ref):
    hi, lo = split2(x)
    return mm(hi, c_ref[0]) + (mm(lo, c_ref[0]) + mm(hi, c_ref[1]))


def dot_left(c_ref, x):
    hi, lo = split2(x)
    return mm(c_ref[0], hi) + (mm(c_ref[0], lo) + mm(c_ref[1], hi))


def unfold(wide):
    return jnp.concatenate([wide[:, r * GY : (r + 1) * GY] for r in range(FOLD)], axis=0)


def fold(tall):
    q = GX // FOLD
    return jnp.concatenate([tall[r * q : (r + 1) * q] for r in range(FOLD)], axis=1)


def step_kernel(
    nt, ns, control, spectrum, perturb_hbm, index, innov, sigma, qc, cxp, cxpt, cy, cyt,
    out, cost_out,
    perturb, flat, send_f, recv_f, inc, table, hi_hot, lo_hot, upd, adj_row, send_a, recv_a,
    part, parts, grad, p_sem, sf_sem, rf_sem, sa_sem, ra_sem, sp_sem, rp_sem,
):
    n = nt * ns
    my_t, my_s = lax.axis_index("tm"), lax.axis_index("space")
    me = my_t * ns + my_s
    slots, members, levels, piece = perturb.shape
    rows = piece // LANES
    pad_rows = send_f.shape[1]
    q, width = GX // FOLD, FOLD * GY
    tiles = width // LANES
    obs = index.shape[1]

    def peer_of(d):
        peer = (me + d) % n
        return peer, (peer // ns, peer % ns)

    load_p = pltpu.make_async_copy(perturb_hbm, perturb, p_sem)
    load_p.start()

    barrier = pltpu.get_barrier_semaphore()

    def greet(d, c):
        pl.semaphore_signal(barrier, inc=1, device_id=peer_of(d)[1], device_id_type=MESH_ID)
        return c

    lax.fori_loop(1, n, greet, 0)

    def wide_of(ref):
        return jnp.concatenate(
            [ref[pl.ds(a, q, stride=tiles), :] for a in range(tiles)], axis=1
        )

    def flat_from(wide):
        for a in range(tiles):
            flat[pl.ds(a, q, stride=tiles), :] = wide[:, a * LANES : (a + 1) * LANES]

    ctl = wide_of(control)
    spec = wide_of(spectrum)
    mid = dot_right(unfold(ctl * spec), cy)
    flat_from(fold(dot_left(cxpt, mid)))
    flat[q * tiles :, :] = jnp.zeros((flat.shape[0] - q * tiles, LANES), F32)
    for s in range(ns):
        send_f[s] = flat[s * rows : s * rows + pad_rows, :].astype(BF16)
    back = 0.5 * jnp.sum(ctl * ctl, axis=0, keepdims=True)
    back = sum(back[:, a * LANES : (a + 1) * LANES] for a in range(tiles))

    pl.semaphore_wait(barrier, n - 1)

    def f_copy(d):
        peer, dev = peer_of(d)
        return pltpu.make_async_remote_copy(
            send_f.at[peer % ns], recv_f.at[me], sf_sem.at[peer], rf_sem.at[me],
            device_id=dev, device_id_type=MESH_ID,
        )

    def start_f(d, c):
        f_copy(d).start()
        return c

    lax.fori_loop(1, n, start_f, 0)
    recv_f[me] = send_f[my_s]

    table[...] = jnp.zeros(table.shape, F32)
    hi_rows = table.shape[1]
    his, los = [], []
    for t in range(slots):
        ix = index[t : t + 1, :]
        level, point = ix // piece, ix % piece
        hi, lo = (point // LANES) * levels + level, point % LANES
        his.append(hi)
        los.append(lo)
        hi_hot[t] = jnp.where(
            lax.broadcasted_iota(jnp.int32, (hi_rows, obs), 0) == hi, 1.0, 0.0
        ).astype(BF16)
        lo_hot[t] = jnp.where(
            lax.broadcasted_iota(jnp.int32, (LANES, obs), 0) == lo, 1.0, 0.0
        ).astype(BF16)
    inc[...] = jnp.zeros(inc.shape, F32)
    load_p.wait()

    def wait_f(d, c):
        src = (me + n - d) % n
        pltpu.make_async_remote_copy(
            send_f.at[0], recv_f.at[src], sf_sem.at[src], rf_sem.at[src],
            device_id=(src // ns, src % ns), device_id_type=MESH_ID,
        ).wait_recv()
        return c

    lax.fori_loop(1, n, wait_f, 0)

    group = 8

    def add_group(g, c):
        fs = [recv_f[g * group + i].astype(F32) for i in range(group)]
        for j in range(rows):
            at = pl.ds(j * LANES, LANES)
            fb = [jnp.broadcast_to(f[j : j + 1, :], (levels, LANES)) for f in fs]
            for t in range(slots):
                total = inc[t, :, at]
                for i in range(group):
                    total = total + perturb[t, g * group + i, :, at].astype(F32) * fb[i]
                inc[t, :, at] = total
        return c

    lax.fori_loop(0, members // group, add_group, 0)

    cost_row = back
    for t in range(slots):
        for j in range(rows):
            table[t, j * levels : (j + 1) * levels, :] = inc[t, :, j * LANES : (j + 1) * LANES]
        three = jnp.concatenate(split3(table[t]), axis=1).T.astype(BF16)
        picked = mm(three, hi_hot[t])
        picked = picked[:LANES] + picked[LANES : 2 * LANES] + picked[2 * LANES :]
        at_lo = lax.broadcasted_iota(jnp.int32, (LANES, obs), 0) == los[t]
        model = jnp.sum(jnp.where(at_lo, picked, 0.0), axis=0, keepdims=True)
        sg = sigma[t : t + 1, :]
        qct = qc[t : t + 1, :]
        rad = jnp.where(qct == 0, 4.0, jnp.where(qct == 1, 2.0, 1.0)).astype(F32)
        scaled = (model - innov[t : t + 1, :]) / sg
        sq = scaled * scaled / (rad * rad)
        cost = 0.5 * rad * rad * jnp.log1p(sq)
        cost_row = cost_row + sum(cost[:, a : a + LANES] for a in range(0, obs, LANES))
        g = scaled / ((1.0 + sq) * sg)
        at_hi = lax.broadcasted_iota(jnp.int32, (hi_rows, obs), 0) == his[t]
        terms = jnp.concatenate(
            [jnp.where(at_hi, p, 0.0).astype(BF16) for p in split3(g)], axis=0
        )
        u = lax.dot_general(
            terms, lo_hot[t], (((1,), (1,)), ((), ())), preferred_element_type=F32
        )
        u = u[:hi_rows] + u[hi_rows : 2 * hi_rows] + u[2 * hi_rows :]
        table[t] = u.astype(BF16).astype(F32)
        for j in range(rows):
            upd[t, :, j * LANES : (j + 1) * LANES] = table[t, j * levels : (j + 1) * levels, :]

    def a_copy(d):
        peer, dev = peer_of(d)
        return pltpu.make_async_remote_copy(
            send_a.at[peer], recv_a.at[me], sa_sem.at[peer], ra_sem.at[me],
            device_id=dev, device_id_type=MESH_ID,
        )

    adj_row[...] = jnp.zeros(adj_row.shape, F32)

    def one_member(d):
        m = (me + d) % n
        for j in range(rows):
            at = pl.ds(j * LANES, LANES)
            z = sum(perturb[t, m, :, at].astype(F32) * upd[t, :, at] for t in range(slots))
            adj_row[j : j + 1, :] = jnp.sum(z, axis=0, keepdims=True)
        send_a[m] = adj_row[...].astype(BF16)

    one_member(1)

    def next_member(d, c):
        one_member(d)
        a_copy(d - 1).start()
        return c

    lax.fori_loop(2, n + 1, next_member, 0)
    recv_a[me] = send_a[me]

    def wait_a(d, c):
        src = (me + n - d) % n
        pltpu.make_async_remote_copy(
            send_a.at[0], recv_a.at[src], sa_sem.at[src], ra_sem.at[src],
            device_id=(src // ns, src % ns), device_id_type=MESH_ID,
        ).wait_recv()
        return c

    lax.fori_loop(1, n, wait_a, 0)

    for s in range(ns):
        whole = sum(recv_a[t * ns + s].astype(F32) for t in range(nt))
        flat[s * rows : (s + 1) * rows, :] = whole[:rows]
    mid = dot_left(cxp, unfold(wide_of(flat)))
    gr = ctl + spec * fold(dot_right(mid, cyt))
    grad[...] = gr
    sq = jnp.sum(gr * gr, axis=0, keepdims=True)
    sq = sum(sq[:, a * LANES : (a + 1) * LANES] for a in range(tiles))
    part[0:1, :] = cost_row
    part[1:2, :] = sq

    def s_copy(d):
        peer, dev = peer_of(d)
        return pltpu.make_async_remote_copy(
            part, parts.at[me], sp_sem.at[peer], rp_sem.at[me],
            device_id=dev, device_id_type=MESH_ID,
        )

    def start_s(d, c):
        s_copy(d).start()
        return c

    lax.fori_loop(1, n, start_s, 0)
    parts[me] = part[...]

    def drain(d, c):
        f_copy(d).wait_send()
        a_copy(d).wait_send()
        return c

    lax.fori_loop(1, n, drain, 0)

    def wait_s(d, c):
        src = (me + n - d) % n
        pltpu.make_async_remote_copy(
            part, parts.at[src], sp_sem.at[src], rp_sem.at[src],
            device_id=(src // ns, src % ns), device_id_type=MESH_ID,
        ).wait_recv()
        return c

    lax.fori_loop(1, n, wait_s, 0)
    sums = jnp.sum(jnp.sum(parts[...], axis=0), axis=1, keepdims=True)
    total_cost, grad_sq = sums[0:1, :], sums[1:2, :]
    step = 0.5 * total_cost / (grad_sq + 1e-06)
    new = ctl - step * grad[...]
    for a in range(tiles):
        out[pl.ds(a, q, stride=tiles), :] = new[:, a * LANES : (a + 1) * LANES]
    cost_out[...] = jnp.broadcast_to(total_cost, cost_out.shape)

    def drain_s(d, c):
        s_copy(d).wait_send()
        return c

    lax.fori_loop(1, n, drain_s, 0)


def fused_device(nt, ns, control, spectrum, perturb, obs_index, innovation, obs_sigma, qc_class):
    n = nt * ns
    slots, members, levels, piece = perturb.shape
    grid_rows = GX * GY // LANES
    rows = piece // LANES
    pad_rows = -(-rows // 16) * 16
    hi_rows = -(-rows * levels // 16) * 16
    obs = obs_index.shape[1]
    vm = pl.BlockSpec(memory_space=pltpu.VMEM)
    dma = pltpu.SemaphoreType.DMA
    bases = [jnp.asarray(b) for b in folded_bases()]
    out, cost = pl.pallas_call(
        functools.partial(step_kernel, nt, ns),
        out_shape=(
            jax.ShapeDtypeStruct((grid_rows, LANES), F32),
            jax.ShapeDtypeStruct((1, LANES), F32),
        ),
        in_specs=[vm, vm, pl.BlockSpec(memory_space=pl.ANY)] + [vm] * 8,
        out_specs=(vm, vm),
        scratch_shapes=[
            pltpu.VMEM(perturb.shape, BF16),
            pltpu.VMEM((grid_rows + 16, LANES), F32),
            pltpu.VMEM((ns, pad_rows, LANES), BF16),
            pltpu.VMEM((n, pad_rows, LANES), BF16),
            pltpu.VMEM((slots, levels, piece), F32),
            pltpu.VMEM((slots, hi_rows, LANES), F32),
            pltpu.VMEM((slots, hi_rows, obs), BF16),
            pltpu.VMEM((slots, LANES, obs), BF16),
            pltpu.VMEM((slots, levels, piece), F32),
            pltpu.VMEM((pad_rows, LANES), F32),
            pltpu.VMEM((n, pad_rows, LANES), BF16),
            pltpu.VMEM((n, pad_rows, LANES), BF16),
            pltpu.VMEM((2, LANES), F32),
            pltpu.VMEM((n, 2, LANES), F32),
            pltpu.VMEM((GX // FOLD, FOLD * GY), F32),
            dma, dma((n,)), dma((n,)), dma((n,)), dma((n,)), dma((n,)), dma((n,)),
        ],
        compiler_params=pltpu.CompilerParams(
            collective_id=0, has_side_effects=True, vmem_limit_bytes=48 << 20
        ),
        name="envar_step",
    )(
        control.reshape(grid_rows, LANES), spectrum.reshape(grid_rows, LANES), perturb,
        obs_index, innovation, obs_sigma, qc_class, *bases,
    )
    return out.reshape(control.shape), cost[0, :1]


def fused_fits(nt, ns, control, perturb, innovation):
    n = nt * ns
    piece = GX * GY // ns
    return (
        control.shape[0] == n
        and piece % LANES == 0
        and (FOLD * GY) % LANES == 0
        and (GX // FOLD) % 8 == 0
        and n % 8 == 0
        and (innovation.shape[1] // ns) % LANES == 0
    )


def solution(mesh):
    nt, ns = mesh.shape["tm"], mesh.shape["space"]

    def whole(control, spectrum, perturb, obs_index, innovation, obs_sigma, qc_class):
        fits = fused_fits(nt, ns, control, perturb, innovation)
        body = functools.partial(fused_device, nt, ns) if fits else per_device
        return on_mesh(mesh, body)(
            control, spectrum, perturb, obs_index, innovation, obs_sigma, qc_class
        )

    return whole


def on_mesh(mesh, body):
    in_specs = (
        P(("tm", "space"), None),
        P(),
        P("tm", None, None, "space"),
        P("tm", "space"),
        P("tm", "space"),
        P("tm", "space"),
        P("tm", "space"),
    )
    out_specs = (P(("tm", "space"), None), P())
    return jax.shard_map(
        body, mesh=mesh, in_specs=in_specs, out_specs=out_specs, check_vma=False
    )
```

```python
import functools

import jax
import jax.numpy as jnp
import ml_dtypes
import numpy as np
from jax import lax
from jax.experimental import pallas as pl
from jax.experimental.pallas import tpu as pltpu
from jax.sharding import PartitionSpec as P

GX = 320
GY = 160


def lookup_tables(segment_length):
    wave_num = jnp.arange(segment_length, dtype=jnp.float32)[:, None]
    grid_positions = jnp.arange(segment_length, dtype=jnp.float32)[None, :]
    basis = jnp.cos(jnp.pi * (grid_positions + 0.5) * wave_num / segment_length) * jnp.sqrt(
        2.0 / segment_length
    )
    return jnp.where(wave_num == 0, basis * jnp.sqrt(0.5), basis)


def synthesize(control, spectrum, basis_x, basis_y):
    coeffs = (control * spectrum[None, :]).reshape(control.shape[0], GX, GY)
    middle = jnp.einsum("kn,mkl->mnl", basis_x, coeffs, precision=lax.Precision.HIGHEST)
    result = jnp.einsum("mnl,lp->mnp", middle, basis_y, precision=lax.Precision.HIGHEST)
    return result.reshape(control.shape[0], GX * GY)


def analyze(adjoint, spectrum, basis_x, basis_y):
    state_fields = adjoint.reshape(adjoint.shape[0], GX, GY)
    middle = jnp.einsum("kn,mnp->mkp", basis_x, state_fields, precision=lax.Precision.HIGHEST)
    result = jnp.einsum("mkp,lp->mkl", middle, basis_y, precision=lax.Precision.HIGHEST)
    return result.reshape(adjoint.shape[0], GX * GY) * spectrum[None, :]


def per_device(control, spectrum, perturb, obs_index, innovation, obs_sigma, qc_class):
    basis_x = lookup_tables(GX)
    basis_y = lookup_tables(GY)
    slot_count = perturb.shape[0]
    levels = perturb.shape[2]
    piece_len = perturb.shape[3]
    radius = jnp.where(qc_class == 0, 4.0, jnp.where(qc_class == 1, 2.0, 1.0)).astype(jnp.float32)

    def scatter_cells(indices, values):
        return jnp.zeros((levels * piece_len,), jnp.float32).at[indices].add(values)

    member_field = synthesize(control, spectrum, basis_x, basis_y).astype(jnp.bfloat16)
    pieces = lax.all_to_all(member_field, "space", split_axis=1, concat_axis=0, tiled=True)
    selected_entries = perturb
    increment = jnp.einsum(
        "dzab,zb->dab",
        selected_entries,
        lax.all_gather(pieces, "tm", axis=0, tiled=True),
        preferred_element_type=jnp.float32,
    )
    cells_flat = increment.reshape(slot_count, levels * piece_len)
    modelled = jnp.take_along_axis(cells_flat, obs_index, axis=1)
    scaled = (modelled - innovation) / obs_sigma
    scaled_sq = scaled * scaled / (radius * radius)
    obs_part = jnp.sum(0.5 * radius * radius * jnp.log1p(scaled_sq))
    back_part = 0.5 * jnp.sum(control * control)
    obs_grad = scaled / ((1.0 + scaled_sq) * obs_sigma)
    control_update = jax.vmap(scatter_cells)(obs_index, obs_grad).astype(jnp.bfloat16)
    control_update = control_update.reshape(slot_count, levels, piece_len)
    selected_entries = perturb
    summed_rows = lax.psum_scatter(
        jnp.einsum(
            "qiyr,qyr->ir", selected_entries, control_update, preferred_element_type=jnp.float32
        ).astype(jnp.bfloat16),
        "tm",
        scatter_dimension=0,
        tiled=True,
    ).astype(jnp.float32)
    adjoint = lax.all_to_all(
        summed_rows.astype(jnp.bfloat16), "space", split_axis=0, concat_axis=1, tiled=True
    ).astype(summed_rows.dtype)
    gradient = control + analyze(adjoint, spectrum, basis_x, basis_y)
    grad_part = jnp.sum(gradient * gradient)
    obs_cost, back_cost = lax.psum((obs_part, back_part), ("tm", "space"))
    grad_sq = lax.psum(grad_part, ("tm", "space"))
    total_cost = back_cost + obs_cost
    step_size = 0.5 * total_cost / (grad_sq + 1e-06)
    control = control - step_size * gradient
    cost_list = [total_cost]
    return (control, jnp.stack(cost_list))


LANES = 128
FOLD = 4
MESH_ID = pl.DeviceIdType.MESH
F32 = jnp.float32
BF16 = jnp.bfloat16


def basis64(n):
    k = np.arange(n, dtype=np.float64)[:, None]
    x = np.arange(n, dtype=np.float64)[None, :]
    c = np.sqrt(2.0 / n) * np.cos(np.pi * (x + 0.5) * k / n)
    c[0] *= np.sqrt(0.5)
    return c.astype(np.float32)


def two_parts(c):
    hi = c.astype(ml_dtypes.bfloat16)
    lo = (c - hi.astype(np.float32)).astype(ml_dtypes.bfloat16)
    return np.stack([hi, lo])


def folded_bases():
    cx, cy = basis64(GX), basis64(GY)
    order = np.arange(GX).reshape(GX // FOLD, FOLD).T.reshape(-1)
    cxp = cx[order][:, order]
    return [two_parts(np.ascontiguousarray(a)) for a in (cxp, cxp.T, cy, cy.T)]


def split2(x):
    hi = x.astype(BF16)
    return hi, (x - hi.astype(F32)).astype(BF16)


def split3(x):
    a = x.astype(BF16).astype(F32)
    b = (x - a).astype(BF16).astype(F32)
    return a, b, x - a - b


def mm(a, b):
    return jnp.dot(a, b, preferred_element_type=F32)


def dot_right(x, c_ref):
    hi, lo = split2(x)
    return mm(hi, c_ref[0]) + (mm(lo, c_ref[0]) + mm(hi, c_ref[1]))


def dot_left(c_ref, x):
    hi, lo = split2(x)
    return mm(c_ref[0], hi) + (mm(c_ref[0], lo) + mm(c_ref[1], hi))


def unfold(wide):
    return jnp.concatenate([wide[:, r * GY : (r + 1) * GY] for r in range(FOLD)], axis=0)


def fold(tall):
    q = GX // FOLD
    return jnp.concatenate([tall[r * q : (r + 1) * q] for r in range(FOLD)], axis=1)


def step_kernel(
    nt, ns, n_in, *refs
):
    sources, (out, cost_out), held = refs[:n_in], refs[n_in : n_in + 2], refs[n_in + 2 :]
    landed, in_sem, held = held[:n_in], held[n_in], held[n_in + 1 :]
    control, spectrum, cy, cxpt, index, perturb, innov, sigma, qc, cxp, cyt = landed
    (
    flat, send_f, recv_f, inc, table, hi_hot, lo_hot, upd, adj_row, send_a, recv_a,
    part, parts, grad, sf_sem, rf_sem, sa_sem, ra_sem, sp_sem, rp_sem,
    ) = held
    n = nt * ns
    my_t, my_s = lax.axis_index("tm"), lax.axis_index("space")
    me = my_t * ns + my_s
    slots, members, levels, piece = perturb.shape
    rows = piece // LANES
    pad_rows = send_f.shape[1]
    q, width = GX // FOLD, FOLD * GY
    tiles = width // LANES
    obs = index.shape[1]

    def peer_of(d):
        peer = (me + d) % n
        return peer, (peer // ns, peer % ns)

    loads = [
        pltpu.make_async_copy(src, dst, in_sem.at[i])
        for i, (src, dst) in enumerate(zip(sources, landed))
    ]
    for load in loads:
        load.start()

    barrier = pltpu.get_barrier_semaphore()

    def greet(d, c):
        pl.semaphore_signal(barrier, inc=1, device_id=peer_of(d)[1], device_id_type=MESH_ID)
        return c

    lax.fori_loop(1, n, greet, 0)

    def wide_of(ref):
        return jnp.concatenate(
            [ref[pl.ds(a, q, stride=tiles), :] for a in range(tiles)], axis=1
        )

    def flat_from(wide):
        for a in range(tiles):
            flat[pl.ds(a, q, stride=tiles), :] = wide[:, a * LANES : (a + 1) * LANES]

    for load in loads[:4]:
        load.wait()
    ctl = wide_of(control)
    spec = wide_of(spectrum)
    mid = dot_right(unfold(ctl * spec), cy)
    flat_from(fold(dot_left(cxpt, mid)))
    flat[q * tiles :, :] = jnp.zeros((flat.shape[0] - q * tiles, LANES), F32)
    for s in range(ns):
        send_f[s] = flat[s * rows : s * rows + pad_rows, :].astype(BF16)
    back = 0.5 * jnp.sum(ctl * ctl, axis=0, keepdims=True)
    back = sum(back[:, a * LANES : (a + 1) * LANES] for a in range(tiles))

    pl.semaphore_wait(barrier, n - 1)

    def f_copy(d):
        peer, dev = peer_of(d)
        return pltpu.make_async_remote_copy(
            send_f.at[peer % ns], recv_f.at[me], sf_sem.at[peer], rf_sem.at[me],
            device_id=dev, device_id_type=MESH_ID,
        )

    def start_f(d, c):
        f_copy(d).start()
        return c

    lax.fori_loop(1, n, start_f, 0)
    recv_f[me] = send_f[my_s]

    loads[4].wait()
    table[...] = jnp.zeros(table.shape, F32)
    hi_rows = table.shape[1]
    his, los = [], []
    for t in range(slots):
        ix = index[t : t + 1, :]
        level, point = ix // piece, ix % piece
        hi, lo = (point // LANES) * levels + level, point % LANES
        his.append(hi)
        los.append(lo)
        hi_hot[t] = jnp.where(
            lax.broadcasted_iota(jnp.int32, (hi_rows, obs), 0) == hi, 1.0, 0.0
        ).astype(BF16)
        lo_hot[t] = jnp.where(
            lax.broadcasted_iota(jnp.int32, (LANES, obs), 0) == lo, 1.0, 0.0
        ).astype(BF16)
    inc[...] = jnp.zeros(inc.shape, F32)
    for load in loads[5:]:
        load.wait()

    def wait_f(d, c):
        src = (me + n - d) % n
        pltpu.make_async_remote_copy(
            send_f.at[0], recv_f.at[src], sf_sem.at[src], rf_sem.at[src],
            device_id=(src // ns, src % ns), device_id_type=MESH_ID,
        ).wait_recv()
        return c

    lax.fori_loop(1, n, wait_f, 0)

    group = 8

    def add_group(g, c):
        fs = [recv_f[g * group + i].astype(F32) for i in range(group)]
        for j in range(rows):
            at = pl.ds(j * LANES, LANES)
            fb = [jnp.broadcast_to(f[j : j + 1, :], (levels, LANES)) for f in fs]
            for t in range(slots):
                total = inc[t, :, at]
                for i in range(group):
                    total = total + perturb[t, g * group + i, :, at].astype(F32) * fb[i]
                inc[t, :, at] = total
        return c

    lax.fori_loop(0, members // group, add_group, 0)

    cost_row = back
    for t in range(slots):
        for j in range(rows):
            table[t, j * levels : (j + 1) * levels, :] = inc[t, :, j * LANES : (j + 1) * LANES]
        three = jnp.concatenate(split3(table[t]), axis=1).T.astype(BF16)
        picked = mm(three, hi_hot[t])
        picked = picked[:LANES] + picked[LANES : 2 * LANES] + picked[2 * LANES :]
        at_lo = lax.broadcasted_iota(jnp.int32, (LANES, obs), 0) == los[t]
        model = jnp.sum(jnp.where(at_lo, picked, 0.0), axis=0, keepdims=True)
        sg = sigma[t : t + 1, :]
        qct = qc[t : t + 1, :]
        rad = jnp.where(qct == 0, 4.0, jnp.where(qct == 1, 2.0, 1.0)).astype(F32)
        scaled = (model - innov[t : t + 1, :]) / sg
        sq = scaled * scaled / (rad * rad)
        cost = 0.5 * rad * rad * jnp.log1p(sq)
        cost_row = cost_row + sum(cost[:, a : a + LANES] for a in range(0, obs, LANES))
        g = scaled / ((1.0 + sq) * sg)
        at_hi = lax.broadcasted_iota(jnp.int32, (hi_rows, obs), 0) == his[t]
        terms = jnp.concatenate(
            [jnp.where(at_hi, p, 0.0).astype(BF16) for p in split3(g)], axis=0
        )
        u = lax.dot_general(
            terms, lo_hot[t], (((1,), (1,)), ((), ())), preferred_element_type=F32
        )
        u = u[:hi_rows] + u[hi_rows : 2 * hi_rows] + u[2 * hi_rows :]
        table[t] = u.astype(BF16).astype(F32)
        for j in range(rows):
            upd[t, :, j * LANES : (j + 1) * LANES] = table[t, j * levels : (j + 1) * levels, :]

    def a_copy(d):
        peer, dev = peer_of(d)
        return pltpu.make_async_remote_copy(
            send_a.at[peer], recv_a.at[me], sa_sem.at[peer], ra_sem.at[me],
            device_id=dev, device_id_type=MESH_ID,
        )

    adj_row[...] = jnp.zeros(adj_row.shape, F32)

    def one_member(d):
        m = (me + d) % n
        for j in range(rows):
            at = pl.ds(j * LANES, LANES)
            z = sum(perturb[t, m, :, at].astype(F32) * upd[t, :, at] for t in range(slots))
            adj_row[j : j + 1, :] = jnp.sum(z, axis=0, keepdims=True)
        send_a[m] = adj_row[...].astype(BF16)

    one_member(1)

    def next_member(d, c):
        one_member(d)
        a_copy(d - 1).start()
        return c

    lax.fori_loop(2, n + 1, next_member, 0)
    recv_a[me] = send_a[me]

    def wait_a(d, c):
        src = (me + n - d) % n
        pltpu.make_async_remote_copy(
            send_a.at[0], recv_a.at[src], sa_sem.at[src], ra_sem.at[src],
            device_id=(src // ns, src % ns), device_id_type=MESH_ID,
        ).wait_recv()
        return c

    lax.fori_loop(1, n, wait_a, 0)

    for s in range(ns):
        whole = sum(recv_a[t * ns + s].astype(F32) for t in range(nt))
        flat[s * rows : (s + 1) * rows, :] = whole[:rows]
    mid = dot_left(cxp, unfold(wide_of(flat)))
    gr = ctl + spec * fold(dot_right(mid, cyt))
    grad[...] = gr
    sq = jnp.sum(gr * gr, axis=0, keepdims=True)
    sq = sum(sq[:, a * LANES : (a + 1) * LANES] for a in range(tiles))
    part[0:1, :] = cost_row
    part[1:2, :] = sq

    def s_copy(d):
        peer, dev = peer_of(d)
        return pltpu.make_async_remote_copy(
            part, parts.at[me], sp_sem.at[peer], rp_sem.at[me],
            device_id=dev, device_id_type=MESH_ID,
        )

    def start_s(d, c):
        s_copy(d).start()
        return c

    lax.fori_loop(1, n, start_s, 0)
    parts[me] = part[...]

    def drain(d, c):
        f_copy(d).wait_send()
        a_copy(d).wait_send()
        return c

    lax.fori_loop(1, n, drain, 0)

    def wait_s(d, c):
        src = (me + n - d) % n
        pltpu.make_async_remote_copy(
            part, parts.at[src], sp_sem.at[src], rp_sem.at[src],
            device_id=(src // ns, src % ns), device_id_type=MESH_ID,
        ).wait_recv()
        return c

    lax.fori_loop(1, n, wait_s, 0)
    sums = jnp.sum(jnp.sum(parts[...], axis=0), axis=1, keepdims=True)
    total_cost, grad_sq = sums[0:1, :], sums[1:2, :]
    step = 0.5 * total_cost / (grad_sq + 1e-06)
    new = ctl - step * grad[...]
    for a in range(tiles):
        out[pl.ds(a, q, stride=tiles), :] = new[:, a * LANES : (a + 1) * LANES]
    cost_out[...] = jnp.broadcast_to(total_cost, cost_out.shape)

    def drain_s(d, c):
        s_copy(d).wait_send()
        return c

    lax.fori_loop(1, n, drain_s, 0)


def fused_device(nt, ns, control, spectrum, perturb, obs_index, innovation, obs_sigma, qc_class):
    n = nt * ns
    slots, members, levels, piece = perturb.shape
    grid_rows = GX * GY // LANES
    rows = piece // LANES
    pad_rows = -(-rows // 16) * 16
    hi_rows = -(-rows * levels // 16) * 16
    obs = obs_index.shape[1]
    vm = pl.BlockSpec(memory_space=pltpu.VMEM)
    dma = pltpu.SemaphoreType.DMA
    cxp, cxpt, cy, cyt = [jnp.asarray(b) for b in folded_bases()]
    sources = [
        control.reshape(grid_rows, LANES), spectrum.reshape(grid_rows, LANES), cy, cxpt,
        obs_index, perturb, innovation, obs_sigma, qc_class, cxp, cyt,
    ]
    out, cost = pl.pallas_call(
        functools.partial(step_kernel, nt, ns, len(sources)),
        out_shape=(
            jax.ShapeDtypeStruct((grid_rows, LANES), F32),
            jax.ShapeDtypeStruct((1, LANES), F32),
        ),
        in_specs=[pl.BlockSpec(memory_space=pltpu.HBM)] * len(sources),
        out_specs=(vm, vm),
        scratch_shapes=[
            *[pltpu.VMEM(a.shape, a.dtype) for a in sources],
            dma((len(sources),)),
            pltpu.VMEM((grid_rows + 16, LANES), F32),
            pltpu.VMEM((ns, pad_rows, LANES), BF16),
            pltpu.VMEM((n, pad_rows, LANES), BF16),
            pltpu.VMEM((slots, levels, piece), F32),
            pltpu.VMEM((slots, hi_rows, LANES), F32),
            pltpu.VMEM((slots, hi_rows, obs), BF16),
            pltpu.VMEM((slots, LANES, obs), BF16),
            pltpu.VMEM((slots, levels, piece), F32),
            pltpu.VMEM((pad_rows, LANES), F32),
            pltpu.VMEM((n, pad_rows, LANES), BF16),
            pltpu.VMEM((n, pad_rows, LANES), BF16),
            pltpu.VMEM((2, LANES), F32),
            pltpu.VMEM((n, 2, LANES), F32),
            pltpu.VMEM((GX // FOLD, FOLD * GY), F32),
            dma((n,)), dma((n,)), dma((n,)), dma((n,)), dma((n,)), dma((n,)),
        ],
        compiler_params=pltpu.CompilerParams(
            collective_id=0, has_side_effects=True, vmem_limit_bytes=67043328
        ),
        name="envar_step",
    )(*sources)
    return out.reshape(control.shape), cost[0, :1]


def fused_fits(nt, ns, control, perturb, innovation):
    n = nt * ns
    piece = GX * GY // ns
    return (
        control.shape[0] == n
        and piece % LANES == 0
        and (FOLD * GY) % LANES == 0
        and (GX // FOLD) % 8 == 0
        and n % 8 == 0
        and (innovation.shape[1] // ns) % LANES == 0
    )


def solution(mesh):
    nt, ns = mesh.shape["tm"], mesh.shape["space"]

    def whole(control, spectrum, perturb, obs_index, innovation, obs_sigma, qc_class):
        fits = fused_fits(nt, ns, control, perturb, innovation)
        body = functools.partial(fused_device, nt, ns) if fits else per_device
        return on_mesh(mesh, body)(
            control, spectrum, perturb, obs_index, innovation, obs_sigma, qc_class
        )

    return whole


def on_mesh(mesh, body):
    in_specs = (
        P(("tm", "space"), None),
        P(),
        P("tm", None, None, "space"),
        P("tm", "space"),
        P("tm", "space"),
        P("tm", "space"),
        P("tm", "space"),
    )
    out_specs = (P(("tm", "space"), None), P())
    return jax.shard_map(
        body, mesh=mesh, in_specs=in_specs, out_specs=out_specs, check_vma=False
    )
```

```python
import functools

import jax
import jax.numpy as jnp
import ml_dtypes
import numpy as np
from jax import lax
from jax.experimental import pallas as pl
from jax.experimental.pallas import tpu as pltpu
from jax.sharding import PartitionSpec as P

GX = 320
GY = 160


def lookup_tables(segment_length):
    wave_num = jnp.arange(segment_length, dtype=jnp.float32)[:, None]
    grid_positions = jnp.arange(segment_length, dtype=jnp.float32)[None, :]
    basis = jnp.cos(jnp.pi * (grid_positions + 0.5) * wave_num / segment_length) * jnp.sqrt(
        2.0 / segment_length
    )
    return jnp.where(wave_num == 0, basis * jnp.sqrt(0.5), basis)


def synthesize(control, spectrum, basis_x, basis_y):
    coeffs = (control * spectrum[None, :]).reshape(control.shape[0], GX, GY)
    middle = jnp.einsum("kn,mkl->mnl", basis_x, coeffs, precision=lax.Precision.HIGHEST)
    result = jnp.einsum("mnl,lp->mnp", middle, basis_y, precision=lax.Precision.HIGHEST)
    return result.reshape(control.shape[0], GX * GY)


def analyze(adjoint, spectrum, basis_x, basis_y):
    state_fields = adjoint.reshape(adjoint.shape[0], GX, GY)
    middle = jnp.einsum("kn,mnp->mkp", basis_x, state_fields, precision=lax.Precision.HIGHEST)
    result = jnp.einsum("mkp,lp->mkl", middle, basis_y, precision=lax.Precision.HIGHEST)
    return result.reshape(adjoint.shape[0], GX * GY) * spectrum[None, :]


def per_device(control, spectrum, perturb, obs_index, innovation, obs_sigma, qc_class):
    basis_x = lookup_tables(GX)
    basis_y = lookup_tables(GY)
    slot_count = perturb.shape[0]
    levels = perturb.shape[2]
    piece_len = perturb.shape[3]
    radius = jnp.where(qc_class == 0, 4.0, jnp.where(qc_class == 1, 2.0, 1.0)).astype(jnp.float32)

    def scatter_cells(indices, values):
        return jnp.zeros((levels * piece_len,), jnp.float32).at[indices].add(values)

    member_field = synthesize(control, spectrum, basis_x, basis_y).astype(jnp.bfloat16)
    pieces = lax.all_to_all(member_field, "space", split_axis=1, concat_axis=0, tiled=True)
    selected_entries = perturb
    increment = jnp.einsum(
        "dzab,zb->dab",
        selected_entries,
        lax.all_gather(pieces, "tm", axis=0, tiled=True),
        preferred_element_type=jnp.float32,
    )
    cells_flat = increment.reshape(slot_count, levels * piece_len)
    modelled = jnp.take_along_axis(cells_flat, obs_index, axis=1)
    scaled = (modelled - innovation) / obs_sigma
    scaled_sq = scaled * scaled / (radius * radius)
    obs_part = jnp.sum(0.5 * radius * radius * jnp.log1p(scaled_sq))
    back_part = 0.5 * jnp.sum(control * control)
    obs_grad = scaled / ((1.0 + scaled_sq) * obs_sigma)
    control_update = jax.vmap(scatter_cells)(obs_index, obs_grad).astype(jnp.bfloat16)
    control_update = control_update.reshape(slot_count, levels, piece_len)
    selected_entries = perturb
    summed_rows = lax.psum_scatter(
        jnp.einsum(
            "qiyr,qyr->ir", selected_entries, control_update, preferred_element_type=jnp.float32
        ).astype(jnp.bfloat16),
        "tm",
        scatter_dimension=0,
        tiled=True,
    ).astype(jnp.float32)
    adjoint = lax.all_to_all(
        summed_rows.astype(jnp.bfloat16), "space", split_axis=0, concat_axis=1, tiled=True
    ).astype(summed_rows.dtype)
    gradient = control + analyze(adjoint, spectrum, basis_x, basis_y)
    grad_part = jnp.sum(gradient * gradient)
    obs_cost, back_cost = lax.psum((obs_part, back_part), ("tm", "space"))
    grad_sq = lax.psum(grad_part, ("tm", "space"))
    total_cost = back_cost + obs_cost
    step_size = 0.5 * total_cost / (grad_sq + 1e-06)
    control = control - step_size * gradient
    cost_list = [total_cost]
    return (control, jnp.stack(cost_list))


LANES = 128
FOLD = 4
MESH_ID = pl.DeviceIdType.MESH
F32 = jnp.float32
BF16 = jnp.bfloat16


def basis64(n):
    k = np.arange(n, dtype=np.float64)[:, None]
    x = np.arange(n, dtype=np.float64)[None, :]
    c = np.sqrt(2.0 / n) * np.cos(np.pi * (x + 0.5) * k / n)
    c[0] *= np.sqrt(0.5)
    return c.astype(np.float32)


def two_parts(c):
    hi = c.astype(ml_dtypes.bfloat16)
    lo = (c - hi.astype(np.float32)).astype(ml_dtypes.bfloat16)
    return np.stack([hi, lo])


def folded_bases():
    cx, cy = basis64(GX), basis64(GY)
    order = np.arange(GX).reshape(GX // FOLD, FOLD).T.reshape(-1)
    cxp = cx[order][:, order]
    return [two_parts(np.ascontiguousarray(a)) for a in (cxp, cxp.T, cy, cy.T)]


def split2(x):
    hi = x.astype(BF16)
    return hi, (x - hi.astype(F32)).astype(BF16)


def split3(x):
    a = x.astype(BF16).astype(F32)
    b = (x - a).astype(BF16).astype(F32)
    return a, b, x - a - b


def mm(a, b):
    return jnp.dot(a, b, preferred_element_type=F32)


def dot_right(x, c_ref):
    hi, lo = split2(x)
    return mm(hi, c_ref[0]) + (mm(lo, c_ref[0]) + mm(hi, c_ref[1]))


def dot_left(c_ref, x):
    hi, lo = split2(x)
    return mm(c_ref[0], hi) + (mm(c_ref[0], lo) + mm(c_ref[1], hi))


def unfold(wide):
    return jnp.concatenate([wide[:, r * GY : (r + 1) * GY] for r in range(FOLD)], axis=0)


def fold(tall):
    q = GX // FOLD
    return jnp.concatenate([tall[r * q : (r + 1) * q] for r in range(FOLD)], axis=1)


def step_kernel(
    nt, ns, n_in, *refs
):
    sources, (out, cost_out), held = refs[:n_in], refs[n_in : n_in + 2], refs[n_in + 2 :]
    landed, in_sem, held = held[:n_in], held[n_in], held[n_in + 1 :]
    control, spectrum, cy, cxpt, index, perturb, innov, sigma, qc, cxp, cyt = landed
    (
    flat, send_f, recv_f, inc, table, hi_hot, lo_hot, upd, adj_row, send_y, mid_a,
    send_a, recv_a, part, parts, grad, sf_sem, rf_sem, sr_sem, sy_sem, ry_sem, sa_sem, ra_sem, sp_sem, rp_sem,
    ) = held
    n = nt * ns
    my_t, my_s = lax.axis_index("tm"), lax.axis_index("space")
    me = my_t * ns + my_s
    slots, members, levels, piece = perturb.shape
    rows = piece // LANES
    pad_rows = send_f.shape[1]
    q, width = GX // FOLD, FOLD * GY
    tiles = width // LANES
    obs = index.shape[1]

    def peer_of(d):
        peer = lax.rem(me + d, n)
        return peer, (lax.div(peer, ns), lax.rem(peer, ns))

    loads = [
        pltpu.make_async_copy(src, dst, in_sem.at[i])
        for i, (src, dst) in enumerate(zip(sources, landed))
    ]
    for load in loads:
        load.start()

    barrier = pltpu.get_barrier_semaphore()

    def greet(d, c):
        pl.semaphore_signal(barrier, inc=1, device_id=peer_of(d)[1], device_id_type=MESH_ID)
        return c

    lax.fori_loop(1, n, greet, 0)

    def wide_of(ref):
        return jnp.concatenate(
            [ref[pl.ds(a, q, stride=tiles), :] for a in range(tiles)], axis=1
        )

    def flat_from(wide):
        for a in range(tiles):
            flat[pl.ds(a, q, stride=tiles), :] = wide[:, a * LANES : (a + 1) * LANES]

    for load in loads[:4]:
        load.wait()
    ctl = wide_of(control)
    spec = wide_of(spectrum)
    mid = dot_right(unfold(ctl * spec), cy)
    flat_from(fold(dot_left(cxpt, mid)))
    flat[q * tiles :, :] = jnp.zeros((flat.shape[0] - q * tiles, LANES), F32)
    for s in range(ns):
        send_f[s] = flat[s * rows : s * rows + pad_rows, :].astype(BF16)
    back = 0.5 * jnp.sum(ctl * ctl, axis=0, keepdims=True)
    back = sum(back[:, a * LANES : (a + 1) * LANES] for a in range(tiles))

    pl.semaphore_wait(barrier, n - 1)

    other = (nt - 1 - my_t, my_s)

    def ahead(d):
        return lax.rem(my_s + d, ns)

    def f_copy(d):
        return pltpu.make_async_remote_copy(
            send_f.at[ahead(d)], recv_f.at[me], sf_sem.at[ahead(d)], rf_sem.at[me],
            device_id=(my_t, ahead(d)), device_id_type=MESH_ID,
        )

    def relay(s):
        slot = my_t * ns + s
        return pltpu.make_async_remote_copy(
            recv_f.at[slot], recv_f.at[slot], sr_sem.at[s], rf_sem.at[slot],
            device_id=other, device_id_type=MESH_ID,
        )

    def start_f(d, c):
        f_copy(d).start()
        return c

    lax.fori_loop(1, ns, start_f, 0)
    recv_f[me] = send_f[my_s]

    loads[4].wait()
    table[...] = jnp.zeros(table.shape, F32)
    hi_rows = table.shape[1]
    his, los = [], []
    for t in range(slots):
        ix = index[t : t + 1, :]
        level, point = ix // piece, ix % piece
        hi, lo = (point // LANES) * levels + level, point % LANES
        his.append(hi)
        los.append(lo)
        hi_hot[t] = jnp.where(
            lax.broadcasted_iota(jnp.int32, (hi_rows, obs), 0) == hi, 1.0, 0.0
        ).astype(BF16)
        lo_hot[t] = jnp.where(
            lax.broadcasted_iota(jnp.int32, (LANES, obs), 0) == lo, 1.0, 0.0
        ).astype(BF16)
    inc[...] = jnp.zeros(inc.shape, F32)
    for load in loads[5:]:
        load.wait()

    def wait_f(slot):
        pltpu.make_async_remote_copy(
            send_f.at[0], recv_f.at[slot], sf_sem.at[0], rf_sem.at[slot],
            device_id=other, device_id_type=MESH_ID,
        ).wait_recv()

    relay(my_s).start()

    def pass_on(d, c):
        s = ahead(ns - d)
        wait_f(my_t * ns + s)
        relay(s).start()
        return c

    lax.fori_loop(1, ns, pass_on, 0)

    group = 8

    def add_group(g, c):
        fs = [recv_f[g * group + i].astype(F32) for i in range(group)]
        for j in range(rows):
            at = pl.ds(j * LANES, LANES)
            fb = [jnp.broadcast_to(f[j : j + 1, :], (levels, LANES)) for f in fs]
            for t in range(slots):
                total = inc[t, :, at]
                for i in range(group):
                    total = total + perturb[t, g * group + i, :, at].astype(F32) * fb[i]
                inc[t, :, at] = total
        return c

    mine, theirs = my_t * (ns // group), (nt - 1 - my_t) * (ns // group)
    lax.fori_loop(0, ns // group, lambda g, c: add_group(mine + g, c), 0)

    def add_theirs(g, c):
        for i in range(group):
            wait_f((theirs + g) * group + i)
        return add_group(theirs + g, c)

    lax.fori_loop(0, ns // group, add_theirs, 0)

    cost_row = back
    for t in range(slots):
        for j in range(rows):
            table[t, j * levels : (j + 1) * levels, :] = inc[t, :, j * LANES : (j + 1) * LANES]
        three = jnp.concatenate(split3(table[t]), axis=1).T.astype(BF16)
        picked = mm(three, hi_hot[t])
        picked = picked[:LANES] + picked[LANES : 2 * LANES] + picked[2 * LANES :]
        at_lo = lax.broadcasted_iota(jnp.int32, (LANES, obs), 0) == los[t]
        model = jnp.sum(jnp.where(at_lo, picked, 0.0), axis=0, keepdims=True)
        sg = sigma[t : t + 1, :]
        qct = qc[t : t + 1, :]
        rad = jnp.where(qct == 0, 4.0, jnp.where(qct == 1, 2.0, 1.0)).astype(F32)
        scaled = (model - innov[t : t + 1, :]) / sg
        sq = scaled * scaled / (rad * rad)
        cost = 0.5 * rad * rad * jnp.log1p(sq)
        cost_row = cost_row + sum(cost[:, a : a + LANES] for a in range(0, obs, LANES))
        g = scaled / ((1.0 + sq) * sg)
        at_hi = lax.broadcasted_iota(jnp.int32, (hi_rows, obs), 0) == his[t]
        terms = jnp.concatenate(
            [jnp.where(at_hi, p, 0.0).astype(BF16) for p in split3(g)], axis=0
        )
        u = lax.dot_general(
            terms, lo_hot[t], (((1,), (1,)), ((), ())), preferred_element_type=F32
        )
        u = u[:hi_rows] + u[hi_rows : 2 * hi_rows] + u[2 * hi_rows :]
        table[t] = u.astype(BF16).astype(F32)
        for j in range(rows):
            upd[t, :, j * LANES : (j + 1) * LANES] = table[t, j * levels : (j + 1) * levels, :]

    def y_copy(d):
        s = ahead(d)
        return pltpu.make_async_remote_copy(
            send_y.at[s], mid_a.at[s], sy_sem.at[s], ry_sem.at[s],
            device_id=other, device_id_type=MESH_ID,
        )

    def a_copy(d):
        return pltpu.make_async_remote_copy(
            send_a.at[ahead(d)], recv_a.at[my_s], sa_sem.at[ahead(d)], ra_sem.at[my_s],
            device_id=(my_t, ahead(d)), device_id_type=MESH_ID,
        )

    adj_row[...] = jnp.zeros(adj_row.shape, F32)

    def one_member(m):
        for j in range(rows):
            at = pl.ds(j * LANES, LANES)
            z = sum(perturb[t, m, :, at].astype(F32) * upd[t, :, at] for t in range(slots))
            adj_row[j : j + 1, :] = jnp.sum(z, axis=0, keepdims=True)

    def to_other(d):
        one_member((nt - 1 - my_t) * ns + ahead(d))
        send_y[ahead(d)] = adj_row[...].astype(BF16)

    def next_other(d, c):
        to_other(d)
        y_copy(d - 1).start()
        return c

    def to_owner(d):
        s = ahead(d)
        one_member(my_t * ns + s)
        y_copy(d).wait_recv()
        send_a[s] = (adj_row[...] + mid_a[s].astype(F32)).astype(BF16)

    def next_owner(d, c):
        to_owner(d)
        a_copy(d - 1).start()
        return c

    to_other(1)
    lax.fori_loop(2, ns + 1, next_other, 0)
    y_copy(ns).start()
    to_owner(1)
    lax.fori_loop(2, ns + 1, next_owner, 0)
    recv_a[my_s] = send_a[my_s]

    def wait_a(d, c):
        src = ahead(ns - d)
        pltpu.make_async_remote_copy(
            send_a.at[0], recv_a.at[src], sa_sem.at[src], ra_sem.at[src],
            device_id=(my_t, src), device_id_type=MESH_ID,
        ).wait_recv()
        return c

    lax.fori_loop(1, ns, wait_a, 0)

    for s in range(ns):
        flat[s * rows : (s + 1) * rows, :] = recv_a[s].astype(F32)[:rows]
    mid = dot_left(cxp, unfold(wide_of(flat)))
    gr = ctl + spec * fold(dot_right(mid, cyt))
    grad[...] = gr
    sq = jnp.sum(gr * gr, axis=0, keepdims=True)
    sq = sum(sq[:, a * LANES : (a + 1) * LANES] for a in range(tiles))
    part[0:1, :] = cost_row
    part[1:2, :] = sq

    def s_copy(d):
        peer, dev = peer_of(d)
        return pltpu.make_async_remote_copy(
            part, parts.at[me], sp_sem.at[peer], rp_sem.at[me],
            device_id=dev, device_id_type=MESH_ID,
        )

    def start_s(d, c):
        s_copy(d).start()
        return c

    lax.fori_loop(1, n, start_s, 0)
    parts[me] = part[...]

    def drain(d, c):
        f_copy(d).wait_send()
        a_copy(d).wait_send()
        return c

    lax.fori_loop(1, ns, drain, 0)

    def drain_y(d, c):
        relay(ahead(d)).wait_send()
        y_copy(d).wait_send()
        return c

    lax.fori_loop(1, ns + 1, drain_y, 0)

    def wait_s(d, c):
        src = lax.rem(me + n - d, n)
        pltpu.make_async_remote_copy(
            part, parts.at[src], sp_sem.at[src], rp_sem.at[src],
            device_id=(lax.div(src, ns), lax.rem(src, ns)), device_id_type=MESH_ID,
        ).wait_recv()
        return c

    lax.fori_loop(1, n, wait_s, 0)
    sums = jnp.sum(jnp.sum(parts[...], axis=0), axis=1, keepdims=True)
    total_cost, grad_sq = sums[0:1, :], sums[1:2, :]
    step = 0.5 * total_cost / (grad_sq + 1e-06)
    new = ctl - step * grad[...]
    for a in range(tiles):
        out[pl.ds(a, q, stride=tiles), :] = new[:, a * LANES : (a + 1) * LANES]
    cost_out[...] = jnp.broadcast_to(total_cost, cost_out.shape)

    def drain_s(d, c):
        s_copy(d).wait_send()
        return c

    lax.fori_loop(1, n, drain_s, 0)


def fused_device(nt, ns, control, spectrum, perturb, obs_index, innovation, obs_sigma, qc_class):
    n = nt * ns
    slots, members, levels, piece = perturb.shape
    grid_rows = GX * GY // LANES
    rows = piece // LANES
    pad_rows = -(-rows // 16) * 16
    hi_rows = -(-rows * levels // 16) * 16
    obs = obs_index.shape[1]
    vm = pl.BlockSpec(memory_space=pltpu.VMEM)
    dma = pltpu.SemaphoreType.DMA
    cxp, cxpt, cy, cyt = [jnp.asarray(b) for b in folded_bases()]
    sources = [
        control.reshape(grid_rows, LANES), spectrum.reshape(grid_rows, LANES), cy, cxpt,
        obs_index, perturb, innovation, obs_sigma, qc_class, cxp, cyt,
    ]
    out, cost = pl.pallas_call(
        functools.partial(step_kernel, nt, ns, len(sources)),
        out_shape=(
            jax.ShapeDtypeStruct((grid_rows, LANES), F32),
            jax.ShapeDtypeStruct((1, LANES), F32),
        ),
        in_specs=[pl.BlockSpec(memory_space=pltpu.HBM)] * len(sources),
        out_specs=(vm, vm),
        scratch_shapes=[
            *[pltpu.VMEM(a.shape, a.dtype) for a in sources],
            dma((len(sources),)),
            pltpu.VMEM((grid_rows + 16, LANES), F32),
            pltpu.VMEM((ns, pad_rows, LANES), BF16),
            pltpu.VMEM((n, pad_rows, LANES), BF16),
            pltpu.VMEM((slots, levels, piece), F32),
            pltpu.VMEM((slots, hi_rows, LANES), F32),
            pltpu.VMEM((slots, hi_rows, obs), BF16),
            pltpu.VMEM((slots, LANES, obs), BF16),
            pltpu.VMEM((slots, levels, piece), F32),
            pltpu.VMEM((pad_rows, LANES), F32),
            *[pltpu.VMEM((ns, pad_rows, LANES), BF16)] * 4,
            pltpu.VMEM((2, LANES), F32),
            pltpu.VMEM((n, 2, LANES), F32),
            pltpu.VMEM((GX // FOLD, FOLD * GY), F32),
            dma((ns,)), dma((n,)), *[dma((ns,))] * 5, dma((n,)), dma((n,)),
        ],
        compiler_params=pltpu.CompilerParams(
            collective_id=0, has_side_effects=True, vmem_limit_bytes=67043328
        ),
        name="envar_step",
    )(*sources)
    return out.reshape(control.shape), cost[0, :1]


def fused_fits(nt, ns, control, perturb, innovation):
    n = nt * ns
    piece = GX * GY // ns
    return (
        nt == 2
        and ns % 8 == 0
        and control.shape[0] == n
        and piece % LANES == 0
        and (FOLD * GY) % LANES == 0
        and (GX // FOLD) % 8 == 0
        and (innovation.shape[1] // ns) % LANES == 0
    )


def solution(mesh):
    nt, ns = mesh.shape["tm"], mesh.shape["space"]

    def whole(control, spectrum, perturb, obs_index, innovation, obs_sigma, qc_class):
        fits = fused_fits(nt, ns, control, perturb, innovation)
        body = functools.partial(fused_device, nt, ns) if fits else per_device
        return on_mesh(mesh, body)(
            control, spectrum, perturb, obs_index, innovation, obs_sigma, qc_class
        )

    return whole


def on_mesh(mesh, body):
    in_specs = (
        P(("tm", "space"), None),
        P(),
        P("tm", None, None, "space"),
        P("tm", "space"),
        P("tm", "space"),
        P("tm", "space"),
        P("tm", "space"),
    )
    out_specs = (P(("tm", "space"), None), P())
    return jax.shard_map(
        body, mesh=mesh, in_specs=in_specs, out_specs=out_specs, check_vma=False
    )
```
